32 devices in a mesh: dom: 8 (over z, x), sub: 4 (over y, core).
Axes of the slice: x: 2, y: 2, z: 4, core: 2. Of those that a mesh axis runs over, the one named last changes fastest.
Arguments:
- unknowns: float32 [9, 56, 4096], P(None, None, ('dom', 'sub')), may hold values from -6 to 6
- jacobians: float32 [3, 9, 9, 4096], P(None, None, None, ('dom', 'sub')), may hold values from -2 to 2
- flux_local: float32 [4, 9, 9, 4096], P(None, None, None, ('dom', 'sub')), may hold values from -2 to 2
- flux_neighbour: float32 [4, 9, 9, 4096], P(None, None, None, ('dom', 'sub')), may hold values from -2 to 2
- stiffness: float32 [3, 56, 56], replicated, may hold values from -0.75 to 0.75
- volume_stiffness: float32 [3, 56, 56], replicated, may hold values from -0.375 to 0.375
- face_proj: float32 [4, 21, 56], replicated, may hold values from -0.75 to 0.75
- lift_back: float32 [4, 56, 21], replicated, may hold values from -0.625 to 0.625
- cluster: int32 [4096], P(('dom', 'sub')), may hold values from 0 to 2, as said below
- adjacent_column_index: int32 [4, 4096], P(None, ('dom', 'sub')), may hold values from 0 to 319, as said below
- neighbour_face: int32 [4, 4096], P(None, ('dom', 'sub')), may hold values from 0 to 3
- sub_sends: int32 [32, 4, 16], P(('dom', 'sub')), may hold values from 0 to 127
- dom_sends: int32 [32, 128], P(('dom', 'sub')), may hold values from 0 to 127
Outputs:
- updated: float32 [9, 56, 4096], P(None, None, ('dom', 'sub'))
The draws below stay inside these ranges and needn't reach their ends.
Inputs may be any that keep to these rules, and one draw needn't show every extreme that they name: On every device the elements are ordered by cluster, never falling; at most 32 of a device's elements are in cluster 0 and at most 64 in clusters 0 and 1; some device has exactly 32 in cluster 0 and some exactly 64 in clusters 0 and 1. `adjacent_column_index`: values below 128 name elements of the same device; each of the 192 columns from 128 on is named by exactly one face of each device.
All inputs are finite; a program needn't handle non-finite values.
Results may differ from the reference program's by a relative error of at most 0.0001.
Values sent between devices are 32-bit elements; how exact they have to be, the bound alone decides.
A program may use at most 128 MiB of HBM per device.

```python
import math
import jax
import jax.numpy as jnp
from jax import lax

QUANT = 9
ORDER = 6
BASIS = 56
FACEB = 21
E_DEV = 128
HS = 16
HD = 64
FINE_CAP = 32
MID_CAP = 64
INCOMING = 192
ELEMS = 4096
N_DOM = 8
N_SUB = 4
DEVICES = 32


def draw_cluster(key, part):
    subkeys = jax.random.split(key, 4)
    position = jnp.arange(DEVICES, dtype=jnp.int32)
    fine_count = jax.random.randint(subkeys[0], (DEVICES,), FINE_CAP // 4, FINE_CAP + 1)
    middle = jax.random.randint(subkeys[1], (DEVICES,), FINE_CAP // 4, MID_CAP + 1)
    chosen_cluster = jax.random.randint(subkeys[2], (), 0, DEVICES)
    second = jax.random.randint(subkeys[3], (), 0, DEVICES)
    fine_count = jnp.where(position == chosen_cluster, FINE_CAP, fine_count)
    upper_count = jnp.minimum(fine_count + middle, MID_CAP)
    upper_count = jnp.where(position == second, MID_CAP, upper_count)
    element_spot = jnp.arange(E_DEV, dtype=jnp.int32)
    labels = jnp.where(element_spot[None, :] < fine_count[:, None], 0, jnp.where(element_spot[None, :] < upper_count[:, None], 1, 2))
    return labels.reshape(-1).astype(jnp.int32)


def draw_adjacent_column_index(key, part):
    subkeys = jax.random.split(key, DEVICES)

    def one_device(device_key):
        first_key, second_key = jax.random.split(device_key)
        local_pick = jax.random.randint(first_key, (4 * E_DEV,), 0, E_DEV)
        shuffled = jax.random.permutation(second_key, 4 * E_DEV)
        filled = local_pick.at[shuffled[:INCOMING]].set(E_DEV + jnp.arange(INCOMING, dtype=jnp.int32))
        return filled.reshape(4, E_DEV)
    stacked = jax.vmap(one_device)(subkeys)
    return jnp.transpose(stacked, (1, 0, 2)).reshape(4, DEVICES * E_DEV).astype(jnp.int32)


def place_ends(values, rng, smallest, top_value):
    place = [jax.random.randint(jax.random.fold_in(rng, axis), (), 0, length) for axis, length in enumerate(values.shape)]
    widest = values.shape.index(max(values.shape))
    next_to = place[:widest] + [(place[widest] + 1) % values.shape[widest]] + place[widest + 1:]
    return values.at[tuple(place)].set(smallest).at[tuple(next_to)].set(top_value)


def block_levels(key, dims, cuts, least, top_value):
    level, own = 1.0, jax.random.fold_in(key, 6)
    for dim, shards_of in cuts:
        steps = jnp.exp(jax.random.uniform(jax.random.fold_in(own, dim), (shards_of,), jnp.float32, least / len(cuts), top_value / len(cuts)))
        level = level * jnp.repeat(steps, dims[dim] // shards_of).reshape([-1 if axis == dim else 1 for axis in range(len(dims))])
    return level


def centred(stream_key, shape, spread, most, cuts=(), kind=jnp.bfloat16):
    array = spread * jax.random.normal(stream_key, shape, jnp.float32)
    if cuts:
        array = array * block_levels(stream_key, shape, cuts, -0.22, 0.18)
    return jnp.clip(array, -most, most).astype(kind)


def setup_inputs(seed: int = 0) -> dict:
    splits = jax.random.split(jax.random.key(seed), 14)
    unknowns = centred(splits[0], (QUANT, BASIS, ELEMS), 1.0, 6.0, ((2, 32),), jnp.float32)
    jacobians = centred(splits[1], (3, QUANT, QUANT, ELEMS), QUANT ** -0.5, 2.0, ((3, 32),), jnp.float32)
    flux_local = centred(splits[2], (4, QUANT, QUANT, ELEMS), QUANT ** -0.5, 2.0, ((3, 32),), jnp.float32)
    flux_neighbour = centred(splits[3], (4, QUANT, QUANT, ELEMS), QUANT ** -0.5, 2.0, ((3, 32),), jnp.float32)
    stiffness = centred(splits[4], (3, BASIS, BASIS), BASIS ** -0.5, 0.75, (), jnp.float32)
    volume_stiffness = centred(splits[5], (3, BASIS, BASIS), (4 * BASIS) ** -0.5, 0.375, (), jnp.float32)
    face_proj = centred(splits[6], (4, FACEB, BASIS), BASIS ** -0.5, 0.75, (), jnp.float32)
    lift_back = centred(splits[7], (4, BASIS, FACEB), (4 * FACEB) ** -0.5, 0.625, (), jnp.float32)
    cluster = draw_cluster(jax.random.fold_in(splits[13], 71), 0)
    adjacent_column_index = draw_adjacent_column_index(jax.random.fold_in(splits[13], 71), 0)
    neighbour_face = place_ends(jax.random.randint(splits[10], (4, ELEMS), 0, 4), jax.random.fold_in(splits[10], 1), 0, 3).astype(jnp.int32)
    sub_sends = place_ends(jax.random.randint(splits[11], (DEVICES, N_SUB, HS), 0, E_DEV), jax.random.fold_in(splits[11], 1), 0, E_DEV - 1).astype(jnp.int32)
    dom_sends = place_ends(jax.random.randint(splits[12], (DEVICES, 2 * HD), 0, E_DEV), jax.random.fold_in(splits[12], 1), 0, E_DEV - 1).astype(jnp.int32)
    return {"unknowns": unknowns, "jacobians": jacobians, "flux_local": flux_local, "flux_neighbour": flux_neighbour, "stiffness": stiffness, "volume_stiffness": volume_stiffness, "face_proj": face_proj, "lift_back": lift_back, "cluster": cluster, "adjacent_column_index": adjacent_column_index, "neighbour_face": neighbour_face, "sub_sends": sub_sends, "dom_sends": dom_sends}


HIGH_PRECISION = lax.Precision.HIGHEST
TICK_LENGTH = 0.25


def taylor_weights():
    return [[TICK_LENGTH ** (polynomial_degree + 1) * ((offset + 1) ** (polynomial_degree + 1) - offset ** (polynomial_degree + 1)) / math.factorial(polynomial_degree + 1) for polynomial_degree in range(ORDER)] for offset in range(4)]


def apply_jacobian(operator_matrix, nodal_values):
    return jnp.sum(operator_matrix[:, :, None, :] * nodal_values[:, None, :, :], axis=0)


def apply_basis(operator_matrix, nodal_values):
    return jnp.einsum('dx,oxz->odz', operator_matrix, nodal_values, precision=HIGH_PRECISION)


def derivative(nodal_values, matrices, jacobians):
    projected = jnp.einsum('dbc,pce->dpbe', matrices, nodal_values, precision=HIGH_PRECISION)
    return jnp.sum(jacobians[:, :, :, None, :] * projected[:, :, None, :, :], axis=(0, 1))


def predict(nodal_values, stiffness, jacobians):
    weights = taylor_weights()
    current = nodal_values
    partials = [weights[offset][0] * current for offset in range(4)]
    for polynomial_degree in range(1, ORDER):
        current = derivative(current, stiffness, jacobians)
        partials = [partials[offset] + weights[offset][polynomial_degree] * current for offset in range(4)]
    return jnp.stack(partials)


def local_flux(own_sum, face_proj, lift_back, flux_local):
    summed = jnp.zeros_like(own_sum)
    for face_slot in range(4):
        trace = apply_basis(face_proj[face_slot], own_sum)
        summed = summed + apply_basis(lift_back[face_slot], apply_jacobian(flux_local[face_slot], trace))
    return summed


def face_traces(nodal_values, face_proj):
    traced = jnp.einsum('jfb,pbr->pfjr', face_proj, nodal_values, precision=HIGH_PRECISION)
    return traced.reshape(traced.shape[0], traced.shape[1], -1)


def neighbour_flux(flattened, selector, lift_back, flux_neighbour):
    summed = None
    for face_slot in range(4):
        gathered = jnp.take(flattened, selector[face_slot], axis=2)
        term = apply_basis(lift_back[face_slot], apply_jacobian(flux_neighbour[face_slot], gathered))
        summed = term if summed is None else summed + term
    return summed


def source_columns(adjacent_column_index, sub_sends, dom_sends):
    column = jnp.arange(ELEMS, dtype=jnp.int32)
    device = column // E_DEV
    dom_index = device // N_SUB
    sub_index = device % N_SUB
    target = adjacent_column_index
    beyond = target - E_DEV
    peer_index = jnp.clip(beyond // HS, 0, N_SUB - 1)
    slot_index = beyond % HS
    sender = dom_index * N_SUB + peer_index
    from_sub = sender * E_DEV + sub_sends[sender, sub_index, slot_index]
    far_slot = beyond - N_SUB * HS
    side_index = jnp.clip(far_slot // HD, 0, 1)
    spot_index = far_slot % HD
    far_device = ((dom_index - 1 + 2 * side_index) % N_DOM) * N_SUB + sub_index
    row_index = jnp.where(side_index == 0, HD + spot_index, spot_index)
    from_dom = far_device * E_DEV + dom_sends[far_device, row_index]
    own_place = device * E_DEV + target
    picked = jnp.where(target < E_DEV, own_place, jnp.where(target < E_DEV + N_SUB * HS, from_sub, from_dom))
    return picked.astype(jnp.int32)


def reference(unknowns, jacobians, flux_local, flux_neighbour, stiffness, volume_stiffness, face_proj, lift_back, cluster, adjacent_column_index, neighbour_face, sub_sends, dom_sends):
    selector = (neighbour_face * ELEMS + source_columns(adjacent_column_index, sub_sends, dom_sends)).astype(jnp.int32)
    length = jnp.where(cluster == 0, 1, jnp.where(cluster == 1, 2, 4)).astype(jnp.int32)
    state = unknowns
    table = jnp.zeros((4,) + unknowns.shape, jnp.float32)
    own_sum = jnp.zeros_like(unknowns)
    flux_sum = jnp.zeros_like(unknowns)
    for tick_number in range(4):
        phases = jnp.remainder(tick_number, length)
        refreshed = phases == 0
        table = jnp.where(refreshed, predict(state, stiffness, jacobians), table)
        pieces = table[0]
        for offset in range(1, 4):
            pieces = jnp.where(phases == offset, table[offset], pieces)
        own_sum = own_sum + pieces
        flattened = face_traces(pieces, face_proj)
        flux_sum = flux_sum + neighbour_flux(flattened, selector, lift_back, flux_neighbour)
        finished = jnp.remainder(tick_number + 1, length) == 0
        change = derivative(own_sum, volume_stiffness, jacobians) - local_flux(own_sum, face_proj, lift_back, flux_local) - flux_sum
        state = jnp.where(finished, state + change, state)
        own_sum = jnp.where(finished, 0.0, own_sum)
        flux_sum = jnp.where(finished, 0.0, flux_sum)
    return state
```

```python
import functools
import math

import jax
import jax.numpy as jnp
from jax import lax
from jax.experimental import pallas as pl
from jax.experimental.pallas import tpu as pltpu
from jax.sharding import PartitionSpec as P

ORDER = 6
TICKS = 4
TICK_LENGTH = 0.25
F32 = jnp.float32
BF16 = jnp.bfloat16
MESH = pl.DeviceIdType.MESH


def taylor_weights(order_count):
    return [
        [
            TICK_LENGTH ** (k + 1) * ((a + 1) ** (k + 1) - a ** (k + 1)) / math.factorial(k + 1)
            for k in range(order_count)
        ]
        for a in range(TICKS)
    ]


def round_up(n, m):
    return -(-n // m) * m


def split(x):
    hi = x.astype(BF16).astype(F32)
    return hi, x - hi


def stacked_rhs(fields):
    blocks = []
    for v in fields:
        hi, lo = split(v)
        blocks.append(jnp.concatenate([hi, lo, hi], axis=0).astype(BF16))
    return jnp.concatenate(blocks, axis=1)


def dot(a, b):
    return jnp.dot(a, b, preferred_element_type=F32)


def kernel(
    sizes,
    u_ref, jac_ref, fl_ref, fn_ref, w_ref, lift_ref, len_ref, adj_ref, nf_ref, send_ref,
    out_ref,
    cur, piece, own, acc_g, proj, tproj, tr, oh, ohs, wl, jin, jrecv, outbuf, arr,
    ssem, rsem, jssem, jrsem,
):
    Q, B, E, FB, n_dom, n_sub, hs, hd = sizes
    R = n_sub * hs + 2 * hd
    RP = arr.shape[1]
    S = n_sub * hs
    nd, ns = 3 * B, 4 * FB
    i_dom, i_sub = lax.axis_index("dom"), lax.axis_index("sub")
    nxt, prv = lax.rem(i_dom + 1, n_dom), lax.rem(i_dom + n_dom - 1, n_dom)
    peers = [lax.rem(i_sub + o, n_sub) for o in range(1, n_sub)]

    barrier = pltpu.get_barrier_semaphore()
    targets = [(i_dom, p) for p in peers] + [(nxt, i_sub), (prv, i_sub)]
    for tgt in targets:
        pl.semaphore_signal(barrier, inc=1, device_id=tgt, device_id_type=MESH)
    pl.semaphore_wait(barrier, len(targets))

    def copies(src, dst, ss, rs):
        made = []
        for o in range(1, n_sub):
            p = peers[o - 1]
            made.append(pltpu.make_async_remote_copy(
                src_ref=src.at[pl.ds(pl.multiple_of(p * hs, 8), hs)],
                dst_ref=dst.at[pl.ds(pl.multiple_of(i_sub * hs, 8), hs)],
                send_sem=ss.at[o - 1], recv_sem=rs.at[o - 1],
                device_id=(i_dom, p), device_id_type=MESH))
        for o, (tgt, a, b) in enumerate([(nxt, S + hd, S), (prv, S, S + hd)]):
            made.append(pltpu.make_async_remote_copy(
                src_ref=src.at[pl.ds(a, hd)], dst_ref=dst.at[pl.ds(b, hd)],
                send_sem=ss.at[n_sub - 1 + o], recv_sem=rs.at[n_sub - 1 + o],
                device_id=(tgt, i_sub), device_id_type=MESH))
        return made

    def self_rows(src, dst):
        rows = pl.ds(pl.multiple_of(i_sub * hs, 8), hs)
        dst[rows, :] = src[rows, :]

    wanted = jnp.zeros((RP, 1), F32)
    for i in range(4):
        adj = adj_ref[pl.ds(i, 1), :]
        nf = nf_ref[pl.ds(i, 1), :]
        key = jnp.where(adj < E, nf * E + adj, -1)
        rows = lax.broadcasted_iota(jnp.int32, (4 * E, E), 0)
        oh[pl.ds(0, 4 * E), pl.ds(i * E, E)] = jnp.where(rows == key, 1.0, 0.0).astype(BF16)
        rows = lax.broadcasted_iota(jnp.int32, (RP, E), 0) + E
        hit = rows == adj
        oh[pl.ds(4 * E, RP), pl.ds(i * E, E)] = jnp.where(hit, 1.0, 0.0).astype(BF16)
        wanted = wanted + jnp.sum(
            jnp.where(hit, nf.astype(F32), 0.0), axis=1, keepdims=True)
    jin[...] = jnp.broadcast_to(wanted[:R], (R, 128))
    first = copies(jin, jrecv, jssem, jrsem)
    for c in first:
        c.start()
    self_rows(jin, jrecv)

    if RP > R:
        for t in range(TICKS):
            arr[t, pl.ds(R, RP - R), :] = jnp.zeros((RP - R, arr.shape[2]), F32)
    out_ref[...] = u_ref[...]
    own[...] = jnp.zeros_like(own)
    acc_g[...] = jnp.zeros_like(acc_g)

    def contract(dst):
        for q0 in range(0, Q, 3):
            sums = [None] * 3
            for d in range(3):
                for p in range(Q):
                    v = proj[pl.ds(d * B, B), pl.ds(p * E, E)]
                    for g in range(3):
                        term = jac_ref[d, p, pl.ds(q0 + g, 1), :] * v
                        sums[g] = term if sums[g] is None else sums[g] + term
            for g in range(3):
                dst(q0 + g, sums[g])

    def put_cur(q, v):
        cur[q] = v

    weights = taylor_weights(ORDER)
    length = len_ref[...]

    def flux(solver, i, trace):
        sums = [None] * Q
        for p in range(Q):
            v = trace(p)
            for q in range(Q):
                term = solver[i, p, pl.ds(q, 1), :] * v
                sums[q] = term if sums[q] is None else sums[q] + term
        return sums

    def tick(t, carry):
        phase = t & (length - 1)
        for k in range(ORDER):
            row = jnp.full((1, E), weights[0][k], F32)
            for a in range(1, TICKS):
                row = jnp.where(phase == a, F32(weights[a][k]), row)
            wl[pl.ds(k, 1), :] = row
        w0 = wl[pl.ds(0, 1), :]
        for p in range(Q):
            v = out_ref[p]
            cur[p] = v
            piece[p] = w0 * v

        def order_step(k, c):
            proj[...] = dot(w_ref[pl.ds(0, nd), :], stacked_rhs([cur[p] for p in range(Q)]))
            wk = wl[pl.ds(k, 1), :]

            def put(q, v):
                cur[q] = v
                piece[q] = piece[q] + wk * v

            contract(put)
            return c

        lax.fori_loop(1, ORDER, order_step, 0)

        tproj[...] = dot(
            w_ref[pl.ds(2 * nd, ns), :], stacked_rhs([piece[p] for p in range(Q)]))
        for p in range(Q):
            for j in range(4):
                tr[pl.ds(p * FB, FB), pl.ds(j * E, E)] = tproj[
                    pl.ds(j * FB, FB), pl.ds(p * E, E)]

        @pl.when(t == 0)
        def _():
            for c in first:
                c.wait()
            want = jrecv[...]
            for j in range(4):
                lane = lax.broadcasted_iota(jnp.int32, (R, E), 1)
                same = jnp.where(lane == send_ref[...], 1.0, 0.0)
                face = jnp.where(want == F32(j), 1.0, 0.0)
                ohs[:, pl.ds(j * E, E)] = (same * face).astype(BF16)

        hi, lo = split(tr[...])
        hi, lo = hi.astype(BF16), lo.astype(BF16)
        nt = (((1,), (1,)), ((), ()))
        o = ohs[...]
        outbuf[t] = (lax.dot_general(o, hi, nt, preferred_element_type=F32)
                     + lax.dot_general(o, lo, nt, preferred_element_type=F32))
        sent = copies(outbuf.at[t], arr.at[t], ssem.at[t], rsem.at[t])
        for c in sent:
            c.start()
        self_rows(outbuf.at[t], arr.at[t])

        for p in range(Q):
            own[p] = own[p] + piece[p]
        rhs = stacked_rhs([own[p] for p in range(Q)])
        proj[...] = dot(w_ref[pl.ds(nd, nd), :], rhs)
        tproj[...] = dot(w_ref[pl.ds(2 * nd, ns), :], rhs)
        contract(put_cur)
        ohl = oh[pl.ds(0, 4 * E), :]
        gathered = dot(hi, ohl) + dot(lo, ohl)

        for c in sent:
            c.wait()
        at = arr[t].T
        ahi, alo = split(at)
        oha = oh[pl.ds(4 * E, RP), :]
        gathered = gathered + dot(ahi.astype(BF16), oha) + dot(alo.astype(BF16), oha)
        tr[...] = gathered

        finished = ((t + 1) & (length - 1)) == 0
        for i in range(4):
            rows = pl.ds(i * FB, FB)
            there = flux(fn_ref, i, lambda p: tr[pl.ds(p * FB, FB), pl.ds(i * E, E)])
            for q in range(Q):
                acc_g[q, rows, :] = acc_g[q, rows, :] + there[q]
            here = flux(fl_ref, i, lambda p: tproj[rows, pl.ds(p * E, E)])
            for q in range(Q):
                proj[rows, pl.ds(q * E, E)] = acc_g[q, rows, :] + here[q]
        lifted = dot(
            lift_ref[...], stacked_rhs([proj[pl.ds(0, ns), pl.ds(q * E, E)] for q in range(Q)]))
        for q in range(Q):
            change = cur[q] - lifted[:, q * E:(q + 1) * E]
            out_ref[q] = jnp.where(finished, out_ref[q] + change, out_ref[q])
            own[q] = jnp.where(finished, 0.0, own[q])
            acc_g[q] = jnp.where(finished, 0.0, acc_g[q])
        return carry

    lax.fori_loop(0, TICKS, tick, 0)


def three_terms(m):
    hi = lax.reduce_precision(m, 8, 7)
    lo = lax.reduce_precision(m - hi, 8, 7)
    return jnp.concatenate([hi, hi, lo], axis=1).astype(BF16)


def local(
    n_dom, n_sub,
    unknowns, jacobians, flux_local, flux_neighbour, stiffness, volume_stiffness,
    face_proj, lift_back, cluster, adjacent_column_index, neighbour_face, sub_sends, dom_sends,
):
    Q, B, E = unknowns.shape
    fb = face_proj.shape[1]
    FB = round_up(fb, 8)
    hs = sub_sends.shape[2]
    hd = dom_sends.shape[1] // 2
    R = n_sub * hs + 2 * hd
    RP = round_up(R, 128)
    pad = ((0, 0), (0, FB - fb), (0, 0))
    w = three_terms(jnp.concatenate([
        stiffness.reshape(3 * B, B), volume_stiffness.reshape(3 * B, B),
        jnp.pad(face_proj, pad).reshape(4 * FB, B)], axis=0))
    lift = three_terms(
        jnp.pad(lift_back.transpose(1, 0, 2), pad[:1] + ((0, 0), (0, FB - fb))).reshape(B, 4 * FB))
    length = jnp.left_shift(1, cluster).astype(jnp.int32).reshape(1, E)
    sends = jnp.concatenate([sub_sends[0].reshape(-1), dom_sends[0]])
    sends = jnp.broadcast_to(sends[:, None], (R, E))
    sizes = (Q, B, E, FB, n_dom, n_sub, hs, hd)
    peers = n_sub + 1
    vm = pl.BlockSpec(memory_space=pltpu.VMEM)
    W = Q * FB
    return pl.pallas_call(
        functools.partial(kernel, sizes),
        out_shape=jax.ShapeDtypeStruct(unknowns.shape, F32),
        in_specs=[vm] * 10,
        out_specs=vm,
        scratch_shapes=[
            pltpu.VMEM((Q, B, E), F32),
            pltpu.VMEM((Q, B, E), F32),
            pltpu.VMEM((Q, B, E), F32),
            pltpu.VMEM((Q, 4 * FB, E), F32),
            pltpu.VMEM((3 * B, Q * E), F32),
            pltpu.VMEM((4 * FB, Q * E), F32),
            pltpu.VMEM((W, 4 * E), F32),
            pltpu.VMEM((4 * E + RP, 4 * E), BF16),
            pltpu.VMEM((R, 4 * E), BF16),
            pltpu.VMEM((8, E), F32),
            pltpu.VMEM((R, 128), F32),
            pltpu.VMEM((R, 128), F32),
            pltpu.VMEM((TICKS, R, W), F32),
            pltpu.VMEM((TICKS, RP, W), F32),
            pltpu.SemaphoreType.DMA((TICKS, peers)),
            pltpu.SemaphoreType.DMA((TICKS, peers)),
            pltpu.SemaphoreType.DMA((peers,)),
            pltpu.SemaphoreType.DMA((peers,)),
        ],
        compiler_params=pltpu.CompilerParams(collective_id=0, has_side_effects=True),
    )(unknowns, jacobians, flux_local, flux_neighbour, w, lift, length,
      adjacent_column_index, neighbour_face, sends)


def solution(mesh):
    both = ("dom", "sub")
    in_specs = (
        P(None, None, both), P(None, None, None, both), P(None, None, None, both),
        P(None, None, None, both), P(), P(), P(), P(), P(both), P(None, both), P(None, both),
        P(both, None, None), P(both, None),
    )
    fn = functools.partial(local, mesh.shape["dom"], mesh.shape["sub"])
    return jax.shard_map(
        fn, mesh=mesh, in_specs=in_specs, out_specs=P(None, None, both), check_vma=False)
```

```python
import functools
import math

import jax
import jax.numpy as jnp
from jax import lax
from jax.experimental import pallas as pl
from jax.experimental.pallas import tpu as pltpu
from jax.sharding import PartitionSpec as P

ORDER = 6
TICKS = 4
TICK_LENGTH = 0.25
F32 = jnp.float32
BF16 = jnp.bfloat16
MESH = pl.DeviceIdType.MESH


def taylor_weights(order_count):
    return [
        [
            TICK_LENGTH ** (k + 1) * ((a + 1) ** (k + 1) - a ** (k + 1)) / math.factorial(k + 1)
            for k in range(order_count)
        ]
        for a in range(TICKS)
    ]


def round_up(n, m):
    return -(-n // m) * m


def split(x):
    hi = x.astype(BF16).astype(F32)
    return hi, x - hi


def stacked_rhs(fields):
    blocks = []
    for v in fields:
        hi, lo = split(v)
        blocks.append(jnp.concatenate([hi, lo, hi], axis=0).astype(BF16))
    return jnp.concatenate(blocks, axis=1)


def dot(a, b):
    return jnp.dot(a, b, preferred_element_type=F32)


def three_terms(m):
    n = m.shape[1]
    hi, lo = split(m)
    row = lax.broadcasted_iota(jnp.int32, (n, 3 * n), 0)
    col = lax.broadcasted_iota(jnp.int32, (n, 3 * n), 1)
    twice = jnp.where((col == row) | (col == row + n), 1.0, 0.0).astype(BF16)
    last = jnp.where(col == row + 2 * n, 1.0, 0.0).astype(BF16)
    return (dot(hi.astype(BF16), twice) + dot(lo.astype(BF16), last)).astype(BF16)


def by_face(ref, width):
    fb, _, b = ref.shape
    rows = []
    for j in range(4):
        rows += [ref[:, j, :], jnp.zeros((width - fb, b), F32)]
    return jnp.concatenate(rows, axis=0)


def kernel(
    sizes,
    u_ref, jac_ref, fl_ref, fn_ref, stiff_ref, vol_ref, fp_ref, lb_ref,
    cluster_ref, adj_ref, nf_ref, sub_ref, dom_ref,
    out_ref,
    w_ref, lift_ref, send_ref,
    cur, piece, own, acc_g, proj, tproj, tr, oh, ohs, wl, jin, jrecv, outbuf, arr,
    ssem, rsem, jssem, jrsem,
):
    Q, B, E, FB, n_dom, n_sub, hs, hd = sizes
    R = n_sub * hs + 2 * hd
    RP = arr.shape[1]
    S = n_sub * hs
    nd, ns = 3 * B, 4 * FB
    i_dom, i_sub = lax.axis_index("dom"), lax.axis_index("sub")
    nxt, prv = lax.rem(i_dom + 1, n_dom), lax.rem(i_dom + n_dom - 1, n_dom)
    peers = [lax.rem(i_sub + o, n_sub) for o in range(1, n_sub)]

    barrier = pltpu.get_barrier_semaphore()
    targets = [(i_dom, p) for p in peers] + [(nxt, i_sub), (prv, i_sub)]
    for tgt in targets:
        pl.semaphore_signal(barrier, inc=1, device_id=tgt, device_id_type=MESH)
    pl.semaphore_wait(barrier, len(targets))

    def copies(src, dst, ss, rs):
        made = []
        for o in range(1, n_sub):
            p = peers[o - 1]
            made.append(pltpu.make_async_remote_copy(
                src_ref=src.at[pl.ds(pl.multiple_of(p * hs, 8), hs)],
                dst_ref=dst.at[pl.ds(pl.multiple_of(i_sub * hs, 8), hs)],
                send_sem=ss.at[o - 1], recv_sem=rs.at[o - 1],
                device_id=(i_dom, p), device_id_type=MESH))
        for o, (tgt, a, b) in enumerate([(nxt, S + hd, S), (prv, S, S + hd)]):
            made.append(pltpu.make_async_remote_copy(
                src_ref=src.at[pl.ds(a, hd)], dst_ref=dst.at[pl.ds(b, hd)],
                send_sem=ss.at[n_sub - 1 + o], recv_sem=rs.at[n_sub - 1 + o],
                device_id=(tgt, i_sub), device_id_type=MESH))
        return made

    def self_rows(src, dst):
        rows = pl.ds(pl.multiple_of(i_sub * hs, 8), hs)
        dst[rows, :] = src[rows, :]

    wanted = jnp.zeros((RP, 1), F32)
    for i in range(4):
        adj = adj_ref[pl.ds(i, 1), :]
        nf = nf_ref[pl.ds(i, 1), :]
        key = jnp.where(adj < E, nf * E + adj, -1)
        rows = lax.broadcasted_iota(jnp.int32, (4 * E, E), 0)
        oh[pl.ds(0, 4 * E), pl.ds(i * E, E)] = jnp.where(rows == key, 1.0, 0.0).astype(BF16)
        rows = lax.broadcasted_iota(jnp.int32, (RP, E), 0) + E
        hit = rows == adj
        oh[pl.ds(4 * E, RP), pl.ds(i * E, E)] = jnp.where(hit, 1.0, 0.0).astype(BF16)
        wanted = wanted + jnp.sum(
            jnp.where(hit, nf.astype(F32), 0.0), axis=1, keepdims=True)
    jin[...] = jnp.broadcast_to(wanted[:R], (R, 128))
    first = copies(jin, jrecv, jssem, jrsem)
    for c in first:
        c.start()
    self_rows(jin, jrecv)

    w_ref[...] = three_terms(jnp.concatenate([
        stiff_ref[...].reshape(nd, B), vol_ref[...].reshape(nd, B),
        by_face(fp_ref, FB)], axis=0))
    back = by_face(lb_ref, FB)
    back = jnp.concatenate([back, jnp.zeros((back.shape[0], 128 - B), F32)], axis=1)
    back = jnp.concatenate([back, jnp.zeros((128 - back.shape[0], 128), F32)], axis=0)
    lift_ref[...] = three_terms(back.T[:B, :ns])

    def column(row):
        n = row.shape[1]
        eye = (lax.broadcasted_iota(jnp.int32, (n, n), 0)
               == lax.broadcasted_iota(jnp.int32, (n, n), 1))
        col = jnp.sum(jnp.where(eye, row.astype(F32), 0.0), axis=1, keepdims=True)
        return jnp.broadcast_to(col, (n, E))

    for p in range(n_sub):
        send_ref[pl.ds(p * hs, hs), :] = column(sub_ref[pl.ds(p, 1), :])
    send_ref[pl.ds(S, 2 * hd), :] = column(dom_ref[...])

    if RP > R:
        for t in range(TICKS):
            arr[t, pl.ds(R, RP - R), :] = jnp.zeros((RP - R, arr.shape[2]), F32)
    out_ref[...] = u_ref[...]
    own[...] = jnp.zeros_like(own)
    acc_g[...] = jnp.zeros_like(acc_g)

    def contract(dst):
        for q0 in range(0, Q, 3):
            sums = [None] * 3
            for d in range(3):
                for p in range(Q):
                    v = proj[pl.ds(d * B, B), pl.ds(p * E, E)]
                    for g in range(3):
                        term = jac_ref[p, q0 + g, pl.ds(d, 1), :] * v
                        sums[g] = term if sums[g] is None else sums[g] + term
            for g in range(3):
                dst(q0 + g, sums[g])

    def put_cur(q, v):
        cur[q] = v

    weights = taylor_weights(ORDER)
    group = cluster_ref[...]
    length = jnp.where(group == 0, 1, jnp.where(group == 1, 2, 4))

    def flux(solver, i, trace):
        sums = [None] * Q
        for p in range(Q):
            v = trace(p)
            for q in range(Q):
                term = solver[p, q, pl.ds(i, 1), :] * v
                sums[q] = term if sums[q] is None else sums[q] + term
        return sums

    def tick(t, carry):
        phase = t & (length - 1)
        for k in range(ORDER):
            row = jnp.full((1, E), weights[0][k], F32)
            for a in range(1, TICKS):
                row = jnp.where(phase == a, F32(weights[a][k]), row)
            wl[pl.ds(k, 1), :] = row
        w0 = wl[pl.ds(0, 1), :]
        for p in range(Q):
            v = out_ref[p]
            cur[p] = v
            piece[p] = w0 * v

        def order_step(k, c):
            proj[...] = dot(w_ref[pl.ds(0, nd), :], stacked_rhs([cur[p] for p in range(Q)]))
            wk = wl[pl.ds(k, 1), :]

            def put(q, v):
                cur[q] = v
                piece[q] = piece[q] + wk * v

            contract(put)
            return c

        lax.fori_loop(1, ORDER, order_step, 0)

        tproj[...] = dot(
            w_ref[pl.ds(2 * nd, ns), :], stacked_rhs([piece[p] for p in range(Q)]))
        for p in range(Q):
            for j in range(4):
                tr[pl.ds(p * FB, FB), pl.ds(j * E, E)] = tproj[
                    pl.ds(j * FB, FB), pl.ds(p * E, E)]

        @pl.when(t == 0)
        def _():
            for c in first:
                c.wait()
            want = jrecv[...]
            for j in range(4):
                lane = lax.broadcasted_iota(jnp.int32, (R, E), 1).astype(F32)
                same = jnp.where(lane == send_ref[...], 1.0, 0.0)
                face = jnp.where(want == F32(j), 1.0, 0.0)
                ohs[:, pl.ds(j * E, E)] = (same * face).astype(BF16)

        hi, lo = split(tr[...])
        hi, lo = hi.astype(BF16), lo.astype(BF16)
        nt = (((1,), (1,)), ((), ()))
        o = ohs[...]
        outbuf[t] = (lax.dot_general(o, hi, nt, preferred_element_type=F32)
                     + lax.dot_general(o, lo, nt, preferred_element_type=F32))
        sent = copies(outbuf.at[t], arr.at[t], ssem.at[t], rsem.at[t])
        for c in sent:
            c.start()
        self_rows(outbuf.at[t], arr.at[t])

        for p in range(Q):
            own[p] = own[p] + piece[p]
        rhs = stacked_rhs([own[p] for p in range(Q)])
        proj[...] = dot(w_ref[pl.ds(nd, nd), :], rhs)
        tproj[...] = dot(w_ref[pl.ds(2 * nd, ns), :], rhs)
        contract(put_cur)
        ohl = oh[pl.ds(0, 4 * E), :]
        gathered = dot(hi, ohl) + dot(lo, ohl)

        for c in sent:
            c.wait()
        at = arr[t].T
        ahi, alo = split(at)
        oha = oh[pl.ds(4 * E, RP), :]
        gathered = gathered + dot(ahi.astype(BF16), oha) + dot(alo.astype(BF16), oha)
        tr[...] = gathered

        finished = ((t + 1) & (length - 1)) == 0
        for i in range(4):
            rows = pl.ds(i * FB, FB)
            there = flux(fn_ref, i, lambda p: tr[pl.ds(p * FB, FB), pl.ds(i * E, E)])
            for q in range(Q):
                acc_g[q, rows, :] = acc_g[q, rows, :] + there[q]
            here = flux(fl_ref, i, lambda p: tproj[rows, pl.ds(p * E, E)])
            for q in range(Q):
                proj[rows, pl.ds(q * E, E)] = acc_g[q, rows, :] + here[q]
        lifted = dot(
            lift_ref[...], stacked_rhs([proj[pl.ds(0, ns), pl.ds(q * E, E)] for q in range(Q)]))
        for q in range(Q):
            change = cur[q] - lifted[:, q * E:(q + 1) * E]
            out_ref[q] = jnp.where(finished, out_ref[q] + change, out_ref[q])
            own[q] = jnp.where(finished, 0.0, own[q])
            acc_g[q] = jnp.where(finished, 0.0, acc_g[q])
        return carry

    lax.fori_loop(0, TICKS, tick, 0)


def local(
    n_dom, n_sub,
    unknowns, jacobians, flux_local, flux_neighbour, stiffness, volume_stiffness,
    face_proj, lift_back, cluster, adjacent_column_index, neighbour_face, sub_sends, dom_sends,
):
    Q, B, E = unknowns.shape
    fb = face_proj.shape[1]
    FB = round_up(fb, 8)
    hs = sub_sends.shape[2]
    hd = dom_sends.shape[1] // 2
    R = n_sub * hs + 2 * hd
    RP = round_up(R, 128)
    sizes = (Q, B, E, FB, n_dom, n_sub, hs, hd)
    peers = n_sub + 1
    vm = pl.BlockSpec(memory_space=pltpu.VMEM)
    W = Q * FB
    return pl.pallas_call(
        functools.partial(kernel, sizes),
        out_shape=jax.ShapeDtypeStruct(unknowns.shape, F32),
        in_specs=[vm] * 13,
        out_specs=vm,
        scratch_shapes=[
            pltpu.VMEM((6 * B + 4 * FB, 3 * B), BF16),
            pltpu.VMEM((B, 12 * FB), BF16),
            pltpu.VMEM((R, E), F32),
            pltpu.VMEM((Q, B, E), F32),
            pltpu.VMEM((Q, B, E), F32),
            pltpu.VMEM((Q, B, E), F32),
            pltpu.VMEM((Q, 4 * FB, E), F32),
            pltpu.VMEM((3 * B, Q * E), F32),
            pltpu.VMEM((4 * FB, Q * E), F32),
            pltpu.VMEM((W, 4 * E), F32),
            pltpu.VMEM((4 * E + RP, 4 * E), BF16),
            pltpu.VMEM((R, 4 * E), BF16),
            pltpu.VMEM((8, E), F32),
            pltpu.VMEM((R, 128), F32),
            pltpu.VMEM((R, 128), F32),
            pltpu.VMEM((TICKS, R, W), F32),
            pltpu.VMEM((TICKS, RP, W), F32),
            pltpu.SemaphoreType.DMA((TICKS, peers)),
            pltpu.SemaphoreType.DMA((TICKS, peers)),
            pltpu.SemaphoreType.DMA((peers,)),
            pltpu.SemaphoreType.DMA((peers,)),
        ],
        compiler_params=pltpu.CompilerParams(collective_id=0, has_side_effects=True),
    )(unknowns, jacobians.transpose(1, 2, 0, 3), flux_local.transpose(1, 2, 0, 3),
      flux_neighbour.transpose(1, 2, 0, 3), stiffness, volume_stiffness,
      face_proj.transpose(1, 0, 2), lift_back.transpose(2, 0, 1), cluster.reshape(1, E),
      adjacent_column_index, neighbour_face, sub_sends[0], dom_sends)


def solution(mesh):
    both = ("dom", "sub")
    in_specs = (
        P(None, None, both), P(None, None, None, both), P(None, None, None, both),
        P(None, None, None, both), P(), P(), P(), P(), P(both), P(None, both), P(None, both),
        P(both, None, None), P(both, None),
    )
    fn = functools.partial(local, mesh.shape["dom"], mesh.shape["sub"])
    return jax.shard_map(
        fn, mesh=mesh, in_specs=in_specs, out_specs=P(None, None, both), check_vma=False)
```

```python
import functools
import math

import jax
import jax.numpy as jnp
from jax import lax
from jax.experimental import pallas as pl
from jax.experimental.pallas import tpu as pltpu
from jax.sharding import PartitionSpec as P

ORDER = 6
TICKS = 4
TICK_LENGTH = 0.25
F32 = jnp.float32
BF16 = jnp.bfloat16
MESH = pl.DeviceIdType.MESH


def taylor_weights(order_count):
    return [
        [
            TICK_LENGTH ** (k + 1) * ((a + 1) ** (k + 1) - a ** (k + 1)) / math.factorial(k + 1)
            for k in range(order_count)
        ]
        for a in range(TICKS)
    ]


def round_up(n, m):
    return -(-n // m) * m


def split(x):
    hi = x.astype(BF16).astype(F32)
    return hi, x - hi


def stacked_rhs(fields):
    blocks = []
    for v in fields:
        hi, lo = split(v)
        blocks.append(jnp.concatenate([hi, lo, hi], axis=0).astype(BF16))
    return jnp.concatenate(blocks, axis=1)


def dot(a, b):
    return jnp.dot(a, b, preferred_element_type=F32)


def three_terms(m):
    n = m.shape[1]
    hi, lo = split(m)
    row = lax.broadcasted_iota(jnp.int32, (n, 3 * n), 0)
    col = lax.broadcasted_iota(jnp.int32, (n, 3 * n), 1)
    twice = jnp.where((col == row) | (col == row + n), 1.0, 0.0).astype(BF16)
    last = jnp.where(col == row + 2 * n, 1.0, 0.0).astype(BF16)
    return (dot(hi.astype(BF16), twice) + dot(lo.astype(BF16), last)).astype(BF16)


def by_face(ref, width):
    fb, _, b = ref.shape
    rows = []
    for j in range(4):
        rows += [ref[:, j, :], jnp.zeros((width - fb, b), F32)]
    return jnp.concatenate(rows, axis=0)


def kernel(
    sizes,
    u_ref, jac_ref, fl_ref, fn_ref, stiff_ref, vol_ref, fp_ref, lb_ref,
    cluster_ref, adj_ref, nf_ref, sub_ref, dom_ref,
    out_ref,
    w_ref, lift_ref, send_ref,
    cur, piece, own, deriv, tacc, proj, tproj, tr, jac2, jac4, fl2, fl4, fn2, fn4, oh, ohs, jin, jrecv, outbuf, arr,
    ssem, rsem, jssem, jrsem,
):
    Q, B, E, FB, n_dom, n_sub, hs, hd = sizes
    R = n_sub * hs + 2 * hd
    RP = arr.shape[1]
    S = n_sub * hs
    nd, ns = 3 * B, 4 * FB
    i_dom, i_sub = lax.axis_index("dom"), lax.axis_index("sub")
    nxt, prv = lax.rem(i_dom + 1, n_dom), lax.rem(i_dom + n_dom - 1, n_dom)
    peers = [lax.rem(i_sub + o, n_sub) for o in range(1, n_sub)]

    barrier = pltpu.get_barrier_semaphore()
    targets = [(i_dom, p) for p in peers] + [(nxt, i_sub), (prv, i_sub)]
    for tgt in targets:
        pl.semaphore_signal(barrier, inc=1, device_id=tgt, device_id_type=MESH)
    pl.semaphore_wait(barrier, len(targets))

    def copies(src, dst, ss, rs):
        made = []
        for o in range(1, n_sub):
            p = peers[o - 1]
            made.append(pltpu.make_async_remote_copy(
                src_ref=src.at[pl.ds(pl.multiple_of(p * hs, 8), hs)],
                dst_ref=dst.at[pl.ds(pl.multiple_of(i_sub * hs, 8), hs)],
                send_sem=ss.at[o - 1], recv_sem=rs.at[o - 1],
                device_id=(i_dom, p), device_id_type=MESH))
        for o, (tgt, a, b) in enumerate([(nxt, S + hd, S), (prv, S, S + hd)]):
            made.append(pltpu.make_async_remote_copy(
                src_ref=src.at[pl.ds(a, hd)], dst_ref=dst.at[pl.ds(b, hd)],
                send_sem=ss.at[n_sub - 1 + o], recv_sem=rs.at[n_sub - 1 + o],
                device_id=(tgt, i_sub), device_id_type=MESH))
        return made

    def self_rows(src, dst):
        rows = pl.ds(pl.multiple_of(i_sub * hs, 8), hs)
        dst[rows, :] = src[rows, :]

    wanted = jnp.zeros((RP, 1), F32)
    for i in range(4):
        adj = adj_ref[pl.ds(i, 1), :]
        nf = nf_ref[pl.ds(i, 1), :]
        key = jnp.where(adj < E, nf * E + adj, -1)
        rows = lax.broadcasted_iota(jnp.int32, (4 * E, E), 0)
        oh[pl.ds(0, 4 * E), pl.ds(i * E, E)] = jnp.where(rows == key, 1.0, 0.0).astype(BF16)
        rows = lax.broadcasted_iota(jnp.int32, (RP, E), 0) + E
        hit = rows == adj
        oh[pl.ds(4 * E, RP), pl.ds(i * E, E)] = jnp.where(hit, 1.0, 0.0).astype(BF16)
        wanted = wanted + jnp.sum(
            jnp.where(hit, nf.astype(F32), 0.0), axis=1, keepdims=True)
    jin[...] = jnp.broadcast_to(wanted[:R], (R, 128))
    first = copies(jin, jrecv, jssem, jrsem)
    for c in first:
        c.start()
    self_rows(jin, jrecv)

    w_ref[...] = three_terms(jnp.concatenate([
        stiff_ref[...].reshape(nd, B), vol_ref[...].reshape(nd, B),
        by_face(fp_ref, FB)], axis=0))
    back = by_face(lb_ref, FB)
    back = jnp.concatenate([back, jnp.zeros((back.shape[0], 128 - B), F32)], axis=1)
    back = jnp.concatenate([back, jnp.zeros((128 - back.shape[0], 128), F32)], axis=0)
    lift_ref[...] = three_terms(back.T[:B, :ns])

    def column(row):
        n = row.shape[1]
        eye = (lax.broadcasted_iota(jnp.int32, (n, n), 0)
               == lax.broadcasted_iota(jnp.int32, (n, n), 1))
        col = jnp.sum(jnp.where(eye, row.astype(F32), 0.0), axis=1, keepdims=True)
        return jnp.broadcast_to(col, (n, E))

    for p in range(n_sub):
        send_ref[pl.ds(p * hs, hs), :] = column(sub_ref[pl.ds(p, 1), :])
    send_ref[pl.ds(S, 2 * hd), :] = column(dom_ref[...])

    if RP > R:
        for t in range(TICKS):
            arr[t, pl.ds(R, RP - R), :] = jnp.zeros((RP - R, arr.shape[2]), F32)
    out_ref[...] = u_ref[...]
    lane = lax.broadcasted_iota(jnp.int32, (1, E), 1)

    def tiles_of(G):
        return -(-Q // G)

    def select(blocks, G):
        w = E // G
        x = blocks[0]
        for g in range(1, G):
            other = blocks[g] if g < len(blocks) else jnp.zeros_like(x)
            x = jnp.where((lane >= g * w) & (lane < (g + 1) * w), other, x)
        return x

    def pack(get, G):
        made = []
        for n in range(tiles_of(G)):
            blocks = []
            for g in range(min(G, Q - G * n)):
                v = get(G * n + g)
                blocks.append(pltpu.roll(v, g * (E // G), 1) if g else v)
            made.append(select(blocks, G))
        return made

    def reduce_groups(v, G):
        while G > 1:
            G //= 2
            v = v + pltpu.roll(v, E // 2 if G == 1 else E // (2 * G), 1)
        return v

    for src, halves, quarters in ((jac_ref, jac2, jac4), (fl_ref, fl2, fl4), (fn_ref, fn2, fn4)):
        for G, dst in ((2, halves), (4, quarters)):
            for q in range(Q):
                for n, v in enumerate(pack(lambda p: src[p, q], G)):
                    dst[n, q] = v
    jacs = {1: jac_ref, 2: jac2, 4: jac4}
    locals_ = {1: fl_ref, 2: fl2, 4: fl4}
    neighbours = {1: fn_ref, 2: fn2, 4: fn4}

    def contract(dst, G):
        jac = jacs[G]
        for q0 in range(0, Q, 3):
            sums = [None] * 3
            for d in range(3):
                for n in range(tiles_of(G)):
                    v = proj[pl.ds(d * B, B), pl.ds(n * E, E)]
                    for g in range(3):
                        term = jac[n, q0 + g, pl.ds(d, 1), :] * v
                        sums[g] = term if sums[g] is None else sums[g] + term
            for g in range(3):
                dst(q0 + g, reduce_groups(sums[g], G))

    weights = taylor_weights(ORDER)
    group = cluster_ref[...]
    length = jnp.where(group == 0, 1, jnp.where(group == 1, 2, 4))

    def predict(G):
        T = tiles_of(G)
        w = E // G
        for n, v in enumerate(pack(lambda p: out_ref[p], G)):
            cur[n] = v

        def order_step(k, c):
            proj[:, pl.ds(0, T * E)] = dot(
                w_ref[pl.ds(0, nd), :], stacked_rhs([cur[n] for n in range(T)]))

            def put(q, v):
                n, g = q // G, q % G
                if G == 1:
                    cur[q] = v
                    deriv[k, q] = v
                    return
                if g == 0:
                    whole = Q - G * n >= G
                    cur[n] = v if whole else jnp.where(lane < w, v, 0.0)
                else:
                    cur[n] = jnp.where((lane >= g * w) & (lane < (g + 1) * w), v, cur[n])
                deriv[k, q] = jnp.where(lane < w, v, deriv[k, q])

            contract(put, G)
            return c

        lax.fori_loop(1, ORDER, order_step, 0)

    def tick(t):
        G_in = {0: 1, 1: 4, 2: 2, 3: 4}[t]
        G = {0: 4, 1: 2, 2: 4, 3: 1}[t]
        T = tiles_of(G)
        w = E // G
        predict(G_in)
        phase = t & (length - 1)
        rows = []
        for k in range(ORDER):
            row = jnp.full((1, E), weights[0][k], F32)
            for a in range(1, TICKS):
                row = jnp.where(phase == a, F32(weights[a][k]), row)
            rows.append(row)
        for p in range(Q):
            v = rows[0] * out_ref[p]
            for k in range(1, ORDER):
                v = v + rows[k] * deriv[k, p]
            piece[p] = v
            own[p] = v if t == 0 else own[p] + v

        tproj[...] = dot(
            w_ref[pl.ds(2 * nd, ns), :], stacked_rhs([piece[p] for p in range(Q)]))
        for p in range(Q):
            for j in range(4):
                tr[pl.ds(p * FB, FB), pl.ds(j * E, E)] = tproj[
                    pl.ds(j * FB, FB), pl.ds(p * E, E)]

        if t == 0:
            for c in first:
                c.wait()
            want = jrecv[...]
            for j in range(4):
                spot = lax.broadcasted_iota(jnp.int32, (R, E), 1).astype(F32)
                same = jnp.where(spot == send_ref[...], 1.0, 0.0)
                face = jnp.where(want == F32(j), 1.0, 0.0)
                ohs[:, pl.ds(j * E, E)] = (same * face).astype(BF16)

        hi, lo = split(tr[...])
        hi, lo = hi.astype(BF16), lo.astype(BF16)
        nt = (((1,), (1,)), ((), ()))
        o = ohs[...]
        outbuf[t] = (lax.dot_general(o, hi, nt, preferred_element_type=F32)
                     + lax.dot_general(o, lo, nt, preferred_element_type=F32))
        sent = copies(outbuf.at[t], arr.at[t], ssem.at[t], rsem.at[t])
        for c in sent:
            c.start()
        self_rows(outbuf.at[t], arr.at[t])

        rhs = stacked_rhs(pack(lambda p: own[p], G))
        proj[:, pl.ds(0, T * E)] = dot(w_ref[pl.ds(nd, nd), :], rhs)
        tproj[:, pl.ds(0, T * E)] = dot(w_ref[pl.ds(2 * nd, ns), :], rhs)

        def put_cur(q, v):
            cur[q] = v

        contract(put_cur, G)
        ohl = oh[pl.ds(0, 4 * E), :]
        gathered = dot(hi, ohl) + dot(lo, ohl)

        for c in sent:
            c.wait()
        at = arr[t].T
        ahi, alo = split(at)
        oha = oh[pl.ds(4 * E, RP), :]
        gathered = gathered + dot(ahi.astype(BF16), oha) + dot(alo.astype(BF16), oha)
        tacc[...] = gathered if t == 0 else tacc[...] + gathered

        for i in range(4):
            rows = pl.ds(i * FB, FB)
            there = pack(lambda p: tacc[pl.ds(p * FB, FB), pl.ds(i * E, E)], G)
            sums = [None] * Q
            for n in range(T):
                here = tproj[rows, pl.ds(n * E, E)]
                for q in range(Q):
                    term = (locals_[G][n, q, pl.ds(i, 1), :] * here
                            + neighbours[G][n, q, pl.ds(i, 1), :] * there[n])
                    sums[q] = term if sums[q] is None else sums[q] + term
            sums = [reduce_groups(v, G) for v in sums]
            for n in range(T):
                proj[rows, pl.ds(n * E, E)] = select(sums[n * G:(n + 1) * G], G)
        lifted = dot(
            lift_ref[...], stacked_rhs([proj[pl.ds(0, ns), pl.ds(n * E, E)] for n in range(T)]))
        finished = ((t + 1) & (length - 1)) == 0
        for q in range(Q):
            n, g = q // G, q % G
            part = lifted[:, n * E:(n + 1) * E]
            if g:
                part = pltpu.roll(part, E - g * w, 1)
            change = cur[q] - part
            if t == TICKS - 1:
                out_ref[q] = out_ref[q] + change
            else:
                out_ref[q] = jnp.where(finished, out_ref[q] + change, out_ref[q])
                own[q] = jnp.where(finished, 0.0, own[q])
        if t < TICKS - 1:
            for i in range(4):
                block = pl.ds(i * E, E)
                tacc[:, block] = jnp.where(finished, 0.0, tacc[:, block])

    for t in range(TICKS):
        tick(t)


def local(
    n_dom, n_sub,
    unknowns, jacobians, flux_local, flux_neighbour, stiffness, volume_stiffness,
    face_proj, lift_back, cluster, adjacent_column_index, neighbour_face, sub_sends, dom_sends,
):
    Q, B, E = unknowns.shape
    fb = face_proj.shape[1]
    FB = round_up(fb, 8)
    hs = sub_sends.shape[2]
    hd = dom_sends.shape[1] // 2
    R = n_sub * hs + 2 * hd
    RP = round_up(R, 128)
    sizes = (Q, B, E, FB, n_dom, n_sub, hs, hd)
    peers = n_sub + 1
    vm = pl.BlockSpec(memory_space=pltpu.VMEM)
    W = Q * FB
    return pl.pallas_call(
        functools.partial(kernel, sizes),
        out_shape=jax.ShapeDtypeStruct(unknowns.shape, F32),
        in_specs=[vm] * 13,
        out_specs=vm,
        scratch_shapes=[
            pltpu.VMEM((6 * B + 4 * FB, 3 * B), BF16),
            pltpu.VMEM((B, 12 * FB), BF16),
            pltpu.VMEM((R, E), F32),
            pltpu.VMEM((Q, B, E), F32),
            pltpu.VMEM((Q, B, E), F32),
            pltpu.VMEM((Q, B, E), F32),
            pltpu.VMEM((ORDER, Q, B, E), F32),
            pltpu.VMEM((W, 4 * E), F32),
            pltpu.VMEM((3 * B, Q * E), F32),
            pltpu.VMEM((4 * FB, Q * E), F32),
            pltpu.VMEM((W, 4 * E), F32),
            pltpu.VMEM((-(-Q // 2), Q, 3, E), F32),
            pltpu.VMEM((-(-Q // 4), Q, 3, E), F32),
            pltpu.VMEM((-(-Q // 2), Q, 4, E), F32),
            pltpu.VMEM((-(-Q // 4), Q, 4, E), F32),
            pltpu.VMEM((-(-Q // 2), Q, 4, E), F32),
            pltpu.VMEM((-(-Q // 4), Q, 4, E), F32),
            pltpu.VMEM((4 * E + RP, 4 * E), BF16),
            pltpu.VMEM((R, 4 * E), BF16),
            pltpu.VMEM((R, 128), F32),
            pltpu.VMEM((R, 128), F32),
            pltpu.VMEM((TICKS, R, W), F32),
            pltpu.VMEM((TICKS, RP, W), F32),
            pltpu.SemaphoreType.DMA((TICKS, peers)),
            pltpu.SemaphoreType.DMA((TICKS, peers)),
            pltpu.SemaphoreType.DMA((peers,)),
            pltpu.SemaphoreType.DMA((peers,)),
        ],
        compiler_params=pltpu.CompilerParams(collective_id=0, has_side_effects=True),
    )(unknowns, jacobians.transpose(1, 2, 0, 3), flux_local.transpose(1, 2, 0, 3),
      flux_neighbour.transpose(1, 2, 0, 3), stiffness, volume_stiffness,
      face_proj.transpose(1, 0, 2), lift_back.transpose(2, 0, 1), cluster.reshape(1, E),
      adjacent_column_index, neighbour_face, sub_sends[0], dom_sends)


def solution(mesh):
    both = ("dom", "sub")
    in_specs = (
        P(None, None, both), P(None, None, None, both), P(None, None, None, both),
        P(None, None, None, both), P(), P(), P(), P(), P(both), P(None, both), P(None, both),
        P(both, None, None), P(both, None),
    )
    fn = functools.partial(local, mesh.shape["dom"], mesh.shape["sub"])
    return jax.shard_map(
        fn, mesh=mesh, in_specs=in_specs, out_specs=P(None, None, both), check_vma=False)
```
